128 devices in a mesh: pix: 8 (over y_hi, x), mode: 16 (over z, y_lo, core).
Axes of the slice: x: 4, y: 4 (y_hi: 2, y_lo: 2; y = y_hi * 2 + y_lo), z: 4, core: 2. Of those that a mesh axis runs over, the one named last changes fastest.
Arguments:
- matrix: float32 [2, 4096, 32768], P(None, 'pix', 'mode'), may hold values from -0.03125 to 0.03125
- calibration_fields: float32 [2, 4096, 512], P(None, 'pix', 'mode'), may hold values from -0.25 to 0.25
- patterns: int32 [32768, 512], P('mode'), may hold values from 0 to 255
- targets: int32 [4096, 128], P('pix'), may hold values from 0 to 255
- phases: float32 [32768, 128], P('mode'), may hold values from -3.140625 to 3.140625
Outputs:
- updated: float32 [2, 4096, 32768], P(None, 'pix', 'mode')
- slm_field: float32 [2, 32768, 128], P(None, 'mode')
- camera_field: float32 [2, 4096, 128], P(None, 'pix')
The draws below stay inside these ranges and needn't reach their ends.
All inputs are finite; a program needn't handle non-finite values.
Results may differ from the reference program's by a relative error of at most 0.00014.
Values sent between devices are 32-bit elements; how exact they have to be, the bound alone decides.
No kernel may reach another device: no remote copies, remote signals or barrier semaphores. Data moves between devices by JAX's collectives and lax.ppermute only.
A program may use at most 128 MiB of HBM per device.

```python
import math
import jax
import jax.numpy as jnp
from jax import lax

PIX = 4096
MODES = 32768
RANK = 512
LEVELS = 256
TARGETS = 128
ITERS = 2


def set_ends(drawn, key, least, top_value):
    longest = drawn.shape.index(max(drawn.shape))
    spots = []
    for shift in (0, 1):
        where = [jax.random.randint(jax.random.fold_in(key, axis), (), 0, length) for axis, length in enumerate(drawn.shape)]
        where[longest] = (where[longest] + shift) % drawn.shape[longest]
        spots.append(tuple(where))
    return drawn.at[spots[0]].set(least).at[spots[1]].set(top_value)


def levels(key, dims, split, low, largest):
    loudness, own = 1.0, jax.random.fold_in(key, 6)
    for axis_at, shards_of in split:
        draws = jnp.exp(jax.random.uniform(jax.random.fold_in(own, axis_at), (shards_of,), jnp.float32, low / len(split), largest / len(split)))
        loudness = loudness * jnp.repeat(draws, dims[axis_at] // shards_of).reshape([-1 if axis == axis_at else 1 for axis in range(len(dims))])
    return loudness


def gaussian(rng, dims, width, most, cuts=(), held_as=jnp.bfloat16):
    result = jax.random.normal(rng, dims, jnp.float32) * width
    if len(cuts) > 0:
        result = levels(rng, dims, cuts, -0.22, 0.18) * result
    return jnp.clip(result, min=-most, max=most).astype(held_as)


def setup_inputs(seed: int = 0) -> dict:
    splits = jax.random.split(jax.random.key(seed), 6)
    return {
        "matrix": gaussian(splits[0], (2, PIX, MODES), MODES ** -0.5, 0.03125, ((1, 8), (2, 16)), jnp.float32),
        "calibration_fields": gaussian(splits[1], (2, PIX, RANK), RANK ** -0.5, 0.25, ((1, 8), (2, 16)), jnp.float32),
        "patterns": set_ends(jax.random.randint(splits[2], (MODES, RANK), 0, LEVELS), jax.random.fold_in(splits[2], 1), 0, LEVELS - 1).astype(jnp.int32),
        "targets": set_ends(jax.random.randint(splits[3], (PIX, TARGETS), 0, 256), jax.random.fold_in(splits[3], 1), 0, 255).astype(jnp.int32),
        "phases": jnp.clip(jax.random.uniform(splits[4], (MODES, TARGETS), jnp.float32, -3.140625, 3.140625), -3.140625, 3.140625),
    }


def matmul(left, right):
    return jnp.dot(left, right, precision=lax.Precision.HIGHEST, preferred_element_type=jnp.float32)

def forward(real_part, imag_part, source):
    return jnp.stack([matmul(real_part, source[0]) - matmul(imag_part, source[1]), matmul(real_part, source[1]) + matmul(imag_part, source[0])])

def adjoint(real_part, imag_part, source):
    return jnp.stack([matmul(real_part.T, source[0]) + matmul(imag_part.T, source[1]), matmul(real_part.T, source[1]) - matmul(imag_part.T, source[0])])

def clamp_scale(source, floor_value):
    magnitude = jnp.sqrt(source[0] * source[0] + source[1] * source[1])
    return 1.0 / jnp.maximum(magnitude, floor_value)

def reference(matrix, calibration_fields, patterns, targets, phases):
    angles = patterns.astype(jnp.float32) * (2.0 * math.pi / LEVELS)
    cosine = jnp.cos(angles) / math.sqrt(MODES)
    sine_table = jnp.sin(angles) / math.sqrt(MODES)
    real_new = matrix[0] + matmul(calibration_fields[0], cosine.T) + matmul(calibration_fields[1], sine_table.T)
    imag_new = matrix[1] + matmul(calibration_fields[1], cosine.T) - matmul(calibration_fields[0], sine_table.T)
    amplitude = targets.astype(jnp.float32) / 128.0
    floor_value = 0.5 * math.sqrt(PIX / MODES)
    slm_now = jnp.stack([jnp.cos(phases), jnp.sin(phases)])
    for repeat in range(ITERS):
        camera = forward(real_new, imag_new, slm_now)
        shaped = camera * (amplitude * clamp_scale(camera, 0.5))
        back_field = adjoint(real_new, imag_new, shaped)
        slm_now = back_field * clamp_scale(back_field, floor_value)
    camera = forward(real_new, imag_new, slm_now)
    return (jnp.stack([real_new, imag_new]), slm_now, camera)
```

```python
import math

import jax
import jax.numpy as jnp
from jax import lax
from jax.sharding import PartitionSpec as P

LEVELS = 256
ITERS = 2
BATCHES = 1


def mm(left, right, dims):
    return lax.dot_general(left, right, (dims, ((), ())), precision=lax.Precision.HIGH, preferred_element_type=jnp.float32)


NN, NT, TN = ((1,), (0,)), ((1,), (1,)), ((0,), (0,))


def pair(real_times, imag_times, width, sign):
    return jnp.concatenate(
        [
            real_times[:, :width] - sign * imag_times[:, width:],
            real_times[:, width:] + sign * imag_times[:, :width],
        ],
        axis=1,
    )


def clamp_scale(source, floor_value, width):
    magnitude = jnp.sqrt(source[:, :width] * source[:, :width] + source[:, width:] * source[:, width:])
    return 1.0 / jnp.maximum(magnitude, floor_value)


def scaled(source, factor):
    return source * jnp.concatenate([factor, factor], axis=1)


def quadrant(turn, rest):
    sq = rest * rest
    sin = rest + rest * sq * (-1.6666654611e-1 + sq * (8.3321608736e-3 - sq * 1.9515295891e-4))
    cos = 1.0 - 0.5 * sq + sq * sq * (4.166664568298827e-2 + sq * (-1.388731625493765e-3 + sq * 2.443315711809948e-5))
    odd = (turn & 1) == 1
    cosine = jnp.where(odd, sin, cos)
    sine = jnp.where(odd, cos, sin)
    cosine = jnp.where(((turn + 1) & 2) == 2, -cosine, cosine)
    sine = jnp.where((turn & 2) == 2, -sine, sine)
    return cosine, sine


def level_wave(levels):
    turn = (levels + LEVELS // 8) // (LEVELS // 4)
    rest = (levels - turn * (LEVELS // 4)).astype(jnp.float32) * (2.0 * math.pi / LEVELS)
    return quadrant(turn, rest)


def phase_wave(phases):
    turns = jnp.round(phases * (2.0 / math.pi))
    rest = (phases - turns * 1.5703125) - turns * (math.pi / 2 - 1.5703125)
    return quadrant(turns.astype(jnp.int32), rest)


def core_groups():
    return [[2 * chip + core for chip in range(8)] for core in range(2)]


def swap_cores(x):
    return lax.ppermute(x, "mode", [(i, i ^ 1) for i in range(16)])


def mode_scatter(x):
    core = lax.axis_index("mode") % 2
    halves = x.reshape(2, x.shape[0] // 2, x.shape[1])
    mine = lax.dynamic_index_in_dim(halves, core, 0, keepdims=False)
    other = lax.dynamic_index_in_dim(halves, 1 - core, 0, keepdims=False)
    mine = mine + swap_cores(other)
    pieces = lax.all_to_all(mine.reshape(8, -1, x.shape[1]), "mode", 0, 0, axis_index_groups=core_groups())
    return jnp.sum(pieces, axis=0)


def mode_gather(x):
    core = lax.axis_index("mode") % 2
    pieces = lax.all_to_all(jnp.broadcast_to(x[None], (8,) + x.shape), "mode", 0, 0, axis_index_groups=core_groups())
    mine = pieces.reshape(-1, x.shape[1])
    other = swap_cores(mine)
    low = jnp.where(core == 0, mine, other)
    high = jnp.where(core == 0, other, mine)
    return jnp.concatenate([low, high], axis=0)


def pix_scatter(x):
    pieces = lax.all_to_all(x.reshape(8, -1, x.shape[1]), "pix", 0, 0)
    return jnp.sum(pieces, axis=0)


def pix_gather(x):
    pieces = lax.all_to_all(jnp.broadcast_to(x[None], (8,) + x.shape), "pix", 0, 0)
    return pieces.reshape(-1, x.shape[1])


def body(matrix, calibration_fields, patterns, targets, phases):
    pix_rows, mode_cols = matrix.shape[1:]
    pix_total = pix_rows * lax.axis_size("pix")
    mode_total = mode_cols * lax.axis_size("mode")
    rank_part = calibration_fields.shape[2]
    width = targets.shape[1] // BATCHES
    floor_value = 0.5 * math.sqrt(pix_total / mode_total)

    fields = jnp.concatenate([calibration_fields[0].T, calibration_fields[1].T], axis=0)
    half = lax.all_to_all(jnp.broadcast_to(fields[None], (8,) + fields.shape), "mode", 0, 0, axis_index_groups=core_groups())
    core = lax.axis_index("mode") % 2
    rest = swap_cores(half)
    low = jnp.where(core == 0, half, rest)
    high = jnp.where(core == 0, rest, half)
    panel = jnp.stack([low, high], axis=1).reshape(16, 2, rank_part, pix_rows)
    field_re = panel[:, 0].reshape(-1, pix_rows)
    field_im = panel[:, 1].reshape(-1, pix_rows)

    cosine, sine = level_wave(patterns)
    cosine, sine = lax.optimization_barrier((cosine / math.sqrt(mode_total), sine / math.sqrt(mode_total)))

    row = (core * 8 + lax.axis_index("mode") // 2) * (pix_rows // 16)
    amplitude = lax.dynamic_slice_in_dim(targets, row, pix_rows // 16, 0).astype(jnp.float32) / 128.0

    slms = []
    firsts = []
    for batch in range(BATCHES):
        ph = phases[:, batch * width : (batch + 1) * width]
        slm = lax.optimization_barrier(jnp.concatenate(phase_wave(ph), axis=1))
        slms.append(slm)
        seen = pair(mm(matrix[0], slm, NN), mm(matrix[1], slm, NN), width, 1.0)
        panel_sum = pair(mm(cosine, slm, TN), mm(sine, slm, TN), width, -1.0)
        seen = seen + pair(mm(field_re, panel_sum, TN), mm(field_im, panel_sum, TN), width, 1.0)
        firsts.append(seen)

    real_new = matrix[0] + (mm(field_re, cosine, ((0,), (1,))) + mm(field_im, sine, ((0,), (1,))))
    imag_new = matrix[1] + (mm(field_im, cosine, ((0,), (1,))) - mm(field_re, sine, ((0,), (1,))))

    cameras = []
    for batch in range(BATCHES):
        slm = slms[batch]
        amp = amplitude[:, batch * width : (batch + 1) * width]
        for repeat in range(ITERS + 1):
            if repeat == 0:
                seen = firsts[batch]
            else:
                seen = pair(mm(real_new, slm, NN), mm(imag_new, slm, NN), width, 1.0)
            seen = mode_scatter(seen)
            if repeat == ITERS:
                cameras.append(mode_gather(seen))
                break
            seen = mode_gather(scaled(seen, amp * clamp_scale(seen, 0.5, width)))
            back = pair(mm(real_new, seen, TN), mm(imag_new, seen, TN), width, -1.0)
            back = pix_scatter(back)
            slm = pix_gather(scaled(back, clamp_scale(back, floor_value, width)))
        slms[batch] = slm
    updated = jnp.stack([real_new, imag_new])
    slm_field = jnp.stack([jnp.concatenate([s[:, k * width : (k + 1) * width] for s in slms], axis=1) for k in range(2)])
    camera_field = jnp.stack([jnp.concatenate([s[:, k * width : (k + 1) * width] for s in cameras], axis=1) for k in range(2)])
    return (updated, slm_field, camera_field)


def solution(mesh):
    in_specs = (
        P(None, "pix", "mode"),
        P(None, "pix", "mode"),
        P("mode", None),
        P("pix", None),
        P("mode", None),
    )
    out_specs = (P(None, "pix", "mode"), P(None, "mode", None), P(None, "pix", None))
    return jax.shard_map(body, mesh=mesh, in_specs=in_specs, out_specs=out_specs, check_vma=False)
```

```python
import functools
import math

import jax
import jax.numpy as jnp
from jax import lax
from jax.experimental import pallas as pl
from jax.experimental.pallas import tpu as pltpu
from jax.sharding import PartitionSpec as P


LEVELS = 256
ITERS = 2
UPDATES = 2


def mm(left, right, dims):
    return lax.dot_general(left, right, (dims, ((), ())), precision=lax.Precision.HIGH, preferred_element_type=jnp.float32)


NN, NT = ((1,), (0,)), ((1,), (1,))


def pair(real_times, imag_times, width, sign):
    return jnp.concatenate(
        [
            real_times[:, :width] - sign * imag_times[:, width:],
            real_times[:, width:] + sign * imag_times[:, :width],
        ],
        axis=1,
    )


def clamp_scale(source, floor_value, width):
    magnitude = jnp.sqrt(source[:, :width] * source[:, :width] + source[:, width:] * source[:, width:])
    return 1.0 / jnp.maximum(magnitude, floor_value)


def scaled(source, factor):
    return source * jnp.concatenate([factor, factor], axis=1)


def quadrant(turn, rest):
    sq = rest * rest
    sin = rest + rest * sq * (-1.6666654611e-1 + sq * (8.3321608736e-3 - sq * 1.9515295891e-4))
    cos = 1.0 - 0.5 * sq + sq * sq * (4.166664568298827e-2 + sq * (-1.388731625493765e-3 + sq * 2.443315711809948e-5))
    odd = (turn & 1) == 1
    cosine = jnp.where(odd, sin, cos)
    sine = jnp.where(odd, cos, sin)
    cosine = jnp.where(((turn + 1) & 2) == 2, -cosine, cosine)
    sine = jnp.where((turn & 2) == 2, -sine, sine)
    return cosine, sine


def level_wave(levels):
    turn = (levels + LEVELS // 8) >> 6
    rest = (levels - (turn << 6)).astype(jnp.float32) * (2.0 * math.pi / LEVELS)
    return quadrant(turn, rest)


def phase_wave(phases):
    turns = jnp.floor(phases * (2.0 / math.pi) + 0.5)
    rest = (phases - turns * 1.5703125) - turns * (math.pi / 2 - 1.5703125)
    return quadrant(turns.astype(jnp.int32), rest)


def split(x):
    high = x.astype(jnp.bfloat16)
    return high, (x - high.astype(jnp.float32)).astype(jnp.bfloat16)


def bdot(left, right, dims):
    return lax.dot_general(left, right, (dims, ((), ())), preferred_element_type=jnp.float32)


def wave_kernel(level_ref, phase_ref, high_ref, low_ref, slm_ref, out_ref, acc_ref):
    step = pl.program_id(0)
    rank = level_ref.shape[1]
    width = phase_ref.shape[1]
    high, low = split(jnp.concatenate(level_wave(level_ref[...]), axis=1))
    high_ref[...] = high
    low_ref[...] = low
    slm = jnp.concatenate(phase_wave(phase_ref[...]), axis=1)
    slm_ref[...] = slm
    slm_high, slm_low = split(slm.T)
    part = bdot(
        jnp.concatenate([slm_high, slm_low, slm_high], axis=1),
        jnp.concatenate([high, high, low], axis=0),
        NN,
    )

    @pl.when(step == 0)
    def _():
        acc_ref[...] = part

    @pl.when(step > 0)
    def _():
        acc_ref[...] += part

    @pl.when(step == pl.num_programs(0) - 1)
    def _():
        out_ref[:width, :] = acc_ref[:width, :rank] + acc_ref[width:, rank:]
        out_ref[width:, :] = acc_ref[width:, :rank] - acc_ref[:width, rank:]


def wave(patterns, phases):
    modes, rank = patterns.shape
    width = phases.shape[1]
    tile = 256
    rows = lambda j: (j, 0)
    return pl.pallas_call(
        wave_kernel,
        name="wave",
        grid=(modes // tile,),
        in_specs=[pl.BlockSpec((tile, rank), rows), pl.BlockSpec((tile, width), rows)],
        out_specs=[
            pl.BlockSpec((tile, 2 * rank), rows),
            pl.BlockSpec((tile, 2 * rank), rows),
            pl.BlockSpec((tile, 2 * width), rows),
            pl.BlockSpec((2 * width, rank), lambda j: (0, 0)),
        ],
        out_shape=[
            jax.ShapeDtypeStruct((modes, 2 * rank), jnp.bfloat16),
            jax.ShapeDtypeStruct((modes, 2 * rank), jnp.bfloat16),
            jax.ShapeDtypeStruct((modes, 2 * width), jnp.float32),
            jax.ShapeDtypeStruct((2 * width, rank), jnp.float32),
        ],
        scratch_shapes=[pltpu.VMEM((2 * width, 2 * rank), jnp.float32)],
        cost_estimate=pl.CostEstimate(flops=8 * 10**9, bytes_accessed=20 * 2**20, transcendentals=0),
    )(patterns, phases)


def first_kernel(scale, core_ref, near_ref, far_ref, sums_ref, seen_ref, out_ref, high_ref, low_ref):
    core = core_ref[0]
    chips, both, _ = near_ref.shape
    part = both // 2
    rank = 2 * chips * part
    width = sums_ref.shape[0] // 2
    for chip in range(chips):
        for ref, side in ((near_ref, core), (far_ref, 1 - core)):
            for plane in range(2):
                row = pl.multiple_of(plane * rank + (2 * chip + side) * part, part)
                high, low = split(ref[chip, plane * part : (plane + 1) * part, :] * scale)
                high_ref[pl.ds(row, part), :] = high
                low_ref[pl.ds(row, part), :] = low
    sums_re = sums_ref[:width, :]
    sums_im = sums_ref[width:, :]
    left = jnp.concatenate(
        [jnp.concatenate([sums_re, -sums_im], axis=1), jnp.concatenate([sums_im, sums_re], axis=1)], axis=0
    )
    left_high, left_low = split(left)
    fields = bdot(left_high, high_ref[...], NN) + (bdot(left_low, high_ref[...], NN) + bdot(left_high, low_ref[...], NN))
    out_ref[...] = seen_ref[...] + fields.T


def first(scale, core, near, far, sums, seen):
    rank2 = 2 * near.shape[0] * near.shape[1]
    pix = near.shape[2]
    vmem = pl.BlockSpec(memory_space=pltpu.VMEM)
    return pl.pallas_call(
        functools.partial(first_kernel, scale),
        name="first",
        in_specs=[pl.BlockSpec(memory_space=pltpu.SMEM)] + [vmem] * 4,
        out_specs=[vmem] * 3,
        out_shape=[
            jax.ShapeDtypeStruct(seen.shape, jnp.float32),
            jax.ShapeDtypeStruct((rank2, pix), jnp.bfloat16),
            jax.ShapeDtypeStruct((rank2, pix), jnp.bfloat16),
        ],
        cost_estimate=pl.CostEstimate(flops=10**9, bytes_accessed=6 * 2**20, transcendentals=0),
    )(core, near, far, sums, seen)


def update_kernel(matrix_ref, high_ref, low_ref, wave_high_ref, wave_low_ref, *refs):
    out_ref, turned_ref, left_ref = refs[-3:]
    rank2, pix = high_ref.shape
    rank = rank2 // 2

    plane = pl.program_id(1)

    @pl.when((pl.program_id(0) == 0) & (plane == 0))
    def _():
        for ref, places in ((high_ref, (0, rank2)), (low_ref, (2 * rank2,))):
            real = ref[:rank, :].astype(jnp.float32).T
            imag = ref[rank:, :].astype(jnp.float32).T
            top = jnp.concatenate([real, imag], axis=1).astype(jnp.bfloat16)
            bottom = jnp.concatenate([imag, -real], axis=1).astype(jnp.bfloat16)
            for place in places:
                left_ref[:pix, place : place + rank2] = top
                left_ref[pix:, place : place + rank2] = bottom

    wave_high = wave_high_ref[...]
    right = jnp.concatenate([wave_high, wave_low_ref[...], wave_high], axis=1)
    rows = pl.ds(pl.multiple_of(plane * pix, pix), pix)
    new = matrix_ref[0] + bdot(left_ref[rows, :], right, NT)
    out_ref[0] = new
    turned_ref[...] = new.T


def update(matrix, high, low, wave_high, wave_low, part, so_far):
    pix, modes = matrix.shape[1:]
    rank2 = high.shape[0]
    tile = 256
    steps = modes // tile // UPDATES
    block = pl.BlockSpec((1, pix, tile), lambda j, plane: (plane, 0, j + part * steps))
    fixed = pl.BlockSpec((rank2, pix), lambda j, plane: (0, 0))
    waves = pl.BlockSpec((tile, rank2), lambda j, plane: (j + part * steps, 0))
    more = [] if so_far is None else list(so_far)
    return pl.pallas_call(
        update_kernel,
        name="update",
        grid=(steps, 2),
        in_specs=[block, fixed, fixed, waves, waves] + [pl.BlockSpec(memory_space=pl.ANY)] * len(more),
        out_specs=[block, pl.BlockSpec((tile, pix), lambda j, plane: (j + part * steps, plane))],
        out_shape=[
            jax.ShapeDtypeStruct(matrix.shape, jnp.float32),
            jax.ShapeDtypeStruct((modes, 2 * pix), jnp.float32),
        ],
        input_output_aliases={5: 0, 6: 1} if more else {},
        scratch_shapes=[pltpu.VMEM((2 * pix, 3 * rank2), jnp.bfloat16)],
        cost_estimate=pl.CostEstimate(
            flops=13 * 10**9 // UPDATES, bytes_accessed=26 * 2**20 // UPDATES, transcendentals=0
        ),
    )(matrix, high, low, wave_high, wave_low, *more)


def core_groups():
    return [[2 * chip + core for chip in range(8)] for core in range(2)]


def swap_cores(x):
    return lax.ppermute(x, "mode", [(i, i ^ 1) for i in range(16)])


def mode_scatter(x):
    core = lax.axis_index("mode") % 2
    halves = x.reshape(2, x.shape[0] // 2, x.shape[1])
    mine = lax.dynamic_index_in_dim(halves, core, 0, keepdims=False)
    other = lax.dynamic_index_in_dim(halves, 1 - core, 0, keepdims=False)
    mine = mine + swap_cores(other)
    pieces = lax.all_to_all(mine.reshape(8, -1, x.shape[1]), "mode", 0, 0, axis_index_groups=core_groups())
    return jnp.sum(pieces, axis=0)


def mode_gather(x):
    core = lax.axis_index("mode") % 2
    copies = jnp.broadcast_to(x[None], (8,) + x.shape)
    pieces = lax.all_to_all(copies, "mode", 0, 0, axis_index_groups=core_groups())
    mine = pieces.reshape(-1, x.shape[1])
    other = swap_cores(mine)
    low = jnp.where(core == 0, mine, other)
    high = jnp.where(core == 0, other, mine)
    return jnp.concatenate([low, high], axis=0)


def swap_pix(x):
    return lax.ppermute(x, "pix", [(i, i ^ 4) for i in range(8)])


def turn_pix(x, shift):
    return lax.ppermute(x, "pix", [(i, (i & 4) + (i + shift) % 4) for i in range(8)])


def pick(x, index, axis):
    return lax.dynamic_index_in_dim(x, index, axis, keepdims=False)


SHIFTS = (1, 3, 2)


def pix_scatter(x):
    place = lax.axis_index("pix")
    y, x_at = place // 4, place % 4
    half = x.shape[1] // 2
    a = x[:, :half].reshape(2, 4, -1, half)
    b = x[:, half:].reshape(2, 4, -1, half)
    b_far = swap_pix(pick(b, 1 - y, 0))
    a_far = [turn_pix(pick(a, (x_at + shift) % 4, 1), shift) for shift in SHIFTS]
    b = pick(b, y, 0) + b_far
    a = pick(a, x_at, 1) + (a_far[0] + a_far[1] + a_far[2])
    b_far = [turn_pix(pick(b, (x_at + shift) % 4, 0), shift) for shift in SHIFTS]
    a_far = swap_pix(pick(a, 1 - y, 0))
    b = pick(b, x_at, 0) + (b_far[0] + b_far[1] + b_far[2])
    a = pick(a, y, 0) + a_far
    return a, b


def by_y(x, far, y):
    return jnp.where(y == 0, jnp.stack([x, far]), jnp.stack([far, x]))


def by_x(x, far, x_at):
    blocks = {0: x}
    for shift, block in zip(SHIFTS, far):
        blocks[-shift % 4] = block
    rows = []
    for k in range(4):
        off = (k - x_at) % 4
        rows.append(jnp.where(off < 2, jnp.where(off == 0, blocks[0], blocks[1]), jnp.where(off == 2, blocks[2], blocks[3])))
    return jnp.stack(rows)


def pix_gather(a, b):
    place = lax.axis_index("pix")
    y, x_at = place // 4, place % 4
    a_far = swap_pix(a)
    b_far = [turn_pix(b, shift) for shift in SHIFTS]
    a = by_y(a, a_far, y)
    b = by_x(b, b_far, x_at)
    b_far = swap_pix(b)
    a_far = [turn_pix(a, shift) for shift in SHIFTS]
    a = by_x(a, a_far, x_at).swapaxes(0, 1)
    b = by_y(b, b_far, y)
    return jnp.concatenate([a.reshape(-1, a.shape[-1]), b.reshape(-1, b.shape[-1])], axis=1)


def planes(matrix, slm):
    width = slm.shape[1] // 2
    pix, modes = matrix.shape[1:]
    times = mm(matrix.reshape(2 * pix, modes), slm, NN)
    return pair(times[:pix], times[pix:], width, 1.0)


def body(matrix, calibration_fields, patterns, targets, phases):
    pix_rows, mode_cols = matrix.shape[1:]
    pix_total = pix_rows * lax.axis_size("pix")
    mode_total = mode_cols * lax.axis_size("mode")
    width = targets.shape[1]
    floor_value = 0.5 * math.sqrt(pix_total / mode_total)

    fields = jnp.concatenate([calibration_fields[0].T, calibration_fields[1].T], axis=0)
    copies = jnp.broadcast_to(fields[None], (8,) + fields.shape)
    half = lax.all_to_all(copies, "mode", 0, 0, axis_index_groups=core_groups())
    core = lax.axis_index("mode") % 2
    rest = swap_cores(half)
    wave_high, wave_low, slm, panel_sum = wave(patterns, phases)

    row = (core * 8 + lax.axis_index("mode") // 2) * (pix_rows // 16)
    amplitude = lax.dynamic_slice_in_dim(targets, row, pix_rows // 16, 0).astype(jnp.float32) / 128.0

    seen = planes(matrix, slm)
    seen, high, low = first(1.0 / math.sqrt(mode_total), core.reshape(1), half, rest, panel_sum, seen)
    parts = None
    for part in range(UPDATES):
        parts = update(matrix, high, low, wave_high, wave_low, part, parts)
    updated, updated_turned = parts

    for repeat in range(ITERS + 1):
        if repeat > 0:
            seen = planes(updated, slm)
        seen = mode_scatter(seen)
        if repeat == ITERS:
            seen = mode_gather(seen)
            break
        seen = mode_gather(scaled(seen, amplitude * clamp_scale(seen, 0.5, width)))
        real, imag = seen[:, :width], seen[:, width:]
        both = jnp.concatenate([seen, jnp.concatenate([imag, -real], axis=1)], axis=0)
        real, imag = pix_scatter(mm(updated_turned, both, NN))
        factor = 1.0 / jnp.maximum(jnp.sqrt(real * real + imag * imag), floor_value)
        slm = pix_gather(real * factor, imag * factor)
    slm_field = jnp.stack([slm[:, :width], slm[:, width:]])
    camera_field = jnp.stack([seen[:, :width], seen[:, width:]])
    return (updated, slm_field, camera_field)


def solution(mesh):
    in_specs = (
        P(None, "pix", "mode"),
        P(None, "pix", "mode"),
        P("mode", None),
        P("pix", None),
        P("mode", None),
    )
    out_specs = (P(None, "pix", "mode"), P(None, "mode", None), P(None, "pix", None))
    return jax.shard_map(body, mesh=mesh, in_specs=in_specs, out_specs=out_specs, check_vma=False)
```

```python
import functools
import math

import jax
import jax.numpy as jnp
from jax import lax
from jax.experimental import pallas as pl
from jax.experimental.pallas import tpu as pltpu
from jax.sharding import PartitionSpec as P


LEVELS = 256
ITERS = 2
UPDATES = 2


def mm(left, right, dims):
    return lax.dot_general(left, right, (dims, ((), ())), precision=lax.Precision.HIGH, preferred_element_type=jnp.float32)


NN, NT = ((1,), (0,)), ((1,), (1,))


def pair(real_times, imag_times, width, sign):
    return jnp.concatenate(
        [
            real_times[:, :width] - sign * imag_times[:, width:],
            real_times[:, width:] + sign * imag_times[:, :width],
        ],
        axis=1,
    )


def clamp_scale(source, floor_value, width):
    magnitude = jnp.sqrt(source[:, :width] * source[:, :width] + source[:, width:] * source[:, width:])
    return 1.0 / jnp.maximum(magnitude, floor_value)


def scaled(source, factor):
    return source * jnp.concatenate([factor, factor], axis=1)


def quadrant(turn, rest):
    sq = rest * rest
    sin = rest + rest * sq * (-1.6666654611e-1 + sq * (8.3321608736e-3 - sq * 1.9515295891e-4))
    cos = 1.0 - 0.5 * sq + sq * sq * (4.166664568298827e-2 + sq * (-1.388731625493765e-3 + sq * 2.443315711809948e-5))
    odd = (turn & 1) == 1
    cosine = jnp.where(odd, sin, cos)
    sine = jnp.where(odd, cos, sin)
    cosine = jnp.where(((turn + 1) & 2) == 2, -cosine, cosine)
    sine = jnp.where((turn & 2) == 2, -sine, sine)
    return cosine, sine


def level_wave(levels):
    turn = (levels + LEVELS // 8) >> 6
    rest = (levels - (turn << 6)).astype(jnp.float32) * (2.0 * math.pi / LEVELS)
    return quadrant(turn, rest)


def phase_wave(phases):
    turns = jnp.floor(phases * (2.0 / math.pi) + 0.5)
    rest = (phases - turns * 1.5703125) - turns * (math.pi / 2 - 1.5703125)
    return quadrant(turns.astype(jnp.int32), rest)


def split(x):
    high = x.astype(jnp.bfloat16)
    return high, (x - high.astype(jnp.float32)).astype(jnp.bfloat16)


def bdot(left, right, dims):
    return lax.dot_general(left, right, (dims, ((), ())), preferred_element_type=jnp.float32)


def wave_kernel(level_ref, phase_ref, high_ref, low_ref, slm_ref, out_ref, acc_ref):
    step = pl.program_id(0)
    rank = level_ref.shape[1]
    width = phase_ref.shape[1]
    high, low = split(jnp.concatenate(level_wave(level_ref[...]), axis=1))
    high_ref[...] = high
    low_ref[...] = low
    slm = jnp.concatenate(phase_wave(phase_ref[...]), axis=1)
    slm_ref[...] = slm
    slm_high, slm_low = split(slm.T)
    part = bdot(
        jnp.concatenate([slm_high, slm_low, slm_high], axis=1),
        jnp.concatenate([high, high, low], axis=0),
        NN,
    )

    @pl.when(step == 0)
    def _():
        acc_ref[...] = part

    @pl.when(step > 0)
    def _():
        acc_ref[...] += part

    @pl.when(step == pl.num_programs(0) - 1)
    def _():
        out_ref[:width, :] = acc_ref[:width, :rank] + acc_ref[width:, rank:]
        out_ref[width:, :] = acc_ref[width:, :rank] - acc_ref[:width, rank:]


def wave(patterns, phases):
    modes, rank = patterns.shape
    width = phases.shape[1]
    tile = 256
    rows = lambda j: (j, 0)
    return pl.pallas_call(
        wave_kernel,
        name="wave",
        grid=(modes // tile,),
        in_specs=[pl.BlockSpec((tile, rank), rows), pl.BlockSpec((tile, width), rows)],
        out_specs=[
            pl.BlockSpec((tile, 2 * rank), rows),
            pl.BlockSpec((tile, 2 * rank), rows),
            pl.BlockSpec((tile, 2 * width), rows),
            pl.BlockSpec((2 * width, rank), lambda j: (0, 0)),
        ],
        out_shape=[
            jax.ShapeDtypeStruct((modes, 2 * rank), jnp.bfloat16),
            jax.ShapeDtypeStruct((modes, 2 * rank), jnp.bfloat16),
            jax.ShapeDtypeStruct((modes, 2 * width), jnp.float32),
            jax.ShapeDtypeStruct((2 * width, rank), jnp.float32),
        ],
        scratch_shapes=[pltpu.VMEM((2 * width, 2 * rank), jnp.float32)],
        cost_estimate=pl.CostEstimate(flops=8 * 10**9, bytes_accessed=20 * 2**20, transcendentals=0),
    )(patterns, phases)


def first_kernel(scale, core_ref, near_ref, far_ref, sums_ref, seen_ref, out_ref, high_ref, low_ref):
    core = core_ref[0]
    chips, both, _ = near_ref.shape
    part = both // 2
    rank = 2 * chips * part
    width = sums_ref.shape[0] // 2
    for chip in range(chips):
        for ref, side in ((near_ref, core), (far_ref, 1 - core)):
            for plane in range(2):
                row = pl.multiple_of(plane * rank + (2 * chip + side) * part, part)
                high, low = split(ref[chip, plane * part : (plane + 1) * part, :] * scale)
                high_ref[pl.ds(row, part), :] = high
                low_ref[pl.ds(row, part), :] = low
    sums_re = sums_ref[:width, :]
    sums_im = sums_ref[width:, :]
    left = jnp.concatenate(
        [jnp.concatenate([sums_re, -sums_im], axis=1), jnp.concatenate([sums_im, sums_re], axis=1)], axis=0
    )
    left_high, left_low = split(left)
    fields = bdot(left_high, high_ref[...], NN) + (bdot(left_low, high_ref[...], NN) + bdot(left_high, low_ref[...], NN))
    out_ref[...] = seen_ref[...] + fields.T


def first(scale, core, near, far, sums, seen):
    rank2 = 2 * near.shape[0] * near.shape[1]
    pix = near.shape[2]
    vmem = pl.BlockSpec(memory_space=pltpu.VMEM)
    return pl.pallas_call(
        functools.partial(first_kernel, scale),
        name="first",
        in_specs=[pl.BlockSpec(memory_space=pltpu.SMEM)] + [vmem] * 4,
        out_specs=[vmem] * 3,
        out_shape=[
            jax.ShapeDtypeStruct(seen.shape, jnp.float32),
            jax.ShapeDtypeStruct((rank2, pix), jnp.bfloat16),
            jax.ShapeDtypeStruct((rank2, pix), jnp.bfloat16),
        ],
        cost_estimate=pl.CostEstimate(flops=10**9, bytes_accessed=6 * 2**20, transcendentals=0),
    )(core, near, far, sums, seen)


def update_kernel(matrix_ref, high_ref, low_ref, wave_high_ref, wave_low_ref, *refs):
    out_ref, turned_ref, left_ref = refs[-3:]
    rank2, pix = high_ref.shape
    rank = rank2 // 2

    @pl.when(pl.program_id(0) == 0)
    def _():
        for ref, places in ((high_ref, (0, rank2)), (low_ref, (2 * rank2,))):
            real = ref[:rank, :].astype(jnp.float32).T
            imag = ref[rank:, :].astype(jnp.float32).T
            top = jnp.concatenate([real, imag], axis=1).astype(jnp.bfloat16)
            bottom = jnp.concatenate([imag, -real], axis=1).astype(jnp.bfloat16)
            for place in places:
                left_ref[:pix, place : place + rank2] = top
                left_ref[pix:, place : place + rank2] = bottom

    wave_high = wave_high_ref[...]
    right = jnp.concatenate([wave_high, wave_low_ref[...], wave_high], axis=1)
    for plane in range(2):
        rows = slice(plane * pix, (plane + 1) * pix)
        new = matrix_ref[plane] + bdot(left_ref[rows, :], right, NT)
        out_ref[plane] = new
        turned_ref[:, rows] = new.T


def update(matrix, high, low, wave_high, wave_low, part, so_far):
    pix, modes = matrix.shape[1:]
    rank2 = high.shape[0]
    tile = 256
    steps = modes // tile // UPDATES
    block = pl.BlockSpec((2, pix, tile), lambda j: (0, 0, j + part * steps))
    fixed = pl.BlockSpec((rank2, pix), lambda j: (0, 0))
    waves = pl.BlockSpec((tile, rank2), lambda j: (j + part * steps, 0))
    more = [] if so_far is None else list(so_far)
    return pl.pallas_call(
        update_kernel,
        name="update",
        grid=(steps,),
        in_specs=[block, fixed, fixed, waves, waves] + [pl.BlockSpec(memory_space=pl.ANY)] * len(more),
        out_specs=[block, pl.BlockSpec((tile, 2 * pix), lambda j: (j + part * steps, 0))],
        out_shape=[
            jax.ShapeDtypeStruct(matrix.shape, jnp.float32),
            jax.ShapeDtypeStruct((modes, 2 * pix), jnp.float32),
        ],
        input_output_aliases={5: 0, 6: 1} if more else {},
        scratch_shapes=[pltpu.VMEM((2 * pix, 3 * rank2), jnp.bfloat16)],
        cost_estimate=pl.CostEstimate(
            flops=13 * 10**9 // UPDATES, bytes_accessed=26 * 2**20 // UPDATES, transcendentals=0
        ),
    )(matrix, high, low, wave_high, wave_low, *more)


def core_groups():
    return [[2 * chip + core for chip in range(8)] for core in range(2)]


def swap_cores(x):
    return lax.ppermute(x, "mode", [(i, i ^ 1) for i in range(16)])


def mode_scatter(x):
    core = lax.axis_index("mode") % 2
    halves = x.reshape(2, x.shape[0] // 2, x.shape[1])
    mine = lax.dynamic_index_in_dim(halves, core, 0, keepdims=False)
    other = lax.dynamic_index_in_dim(halves, 1 - core, 0, keepdims=False)
    mine = mine + swap_cores(other)
    pieces = lax.all_to_all(mine.reshape(8, -1, x.shape[1]), "mode", 0, 0, axis_index_groups=core_groups())
    return jnp.sum(pieces, axis=0)


def mode_gather(x):
    core = lax.axis_index("mode") % 2
    copies = jnp.broadcast_to(x[None], (8,) + x.shape)
    pieces = lax.all_to_all(copies, "mode", 0, 0, axis_index_groups=core_groups())
    mine = pieces.reshape(-1, x.shape[1])
    other = swap_cores(mine)
    low = jnp.where(core == 0, mine, other)
    high = jnp.where(core == 0, other, mine)
    return jnp.concatenate([low, high], axis=0)


def swap_pix(x):
    return lax.ppermute(x, "pix", [(i, i ^ 4) for i in range(8)])


def turn_pix(x, shift):
    return lax.ppermute(x, "pix", [(i, (i & 4) + (i + shift) % 4) for i in range(8)])


def pick(x, index, axis):
    return lax.dynamic_index_in_dim(x, index, axis, keepdims=False)


SHIFTS = (1, 3, 2)


def pix_scatter(x):
    place = lax.axis_index("pix")
    y, x_at = place // 4, place % 4
    half = x.shape[1] // 2
    a = x[:, :half].reshape(2, 4, -1, half)
    b = x[:, half:].reshape(2, 4, -1, half)
    b_far = swap_pix(pick(b, 1 - y, 0))
    a_far = [turn_pix(pick(a, (x_at + shift) % 4, 1), shift) for shift in SHIFTS]
    b = pick(b, y, 0) + b_far
    a = pick(a, x_at, 1) + (a_far[0] + a_far[1] + a_far[2])
    b_far = [turn_pix(pick(b, (x_at + shift) % 4, 0), shift) for shift in SHIFTS]
    a_far = swap_pix(pick(a, 1 - y, 0))
    b = pick(b, x_at, 0) + (b_far[0] + b_far[1] + b_far[2])
    a = pick(a, y, 0) + a_far
    return a, b


def by_y(x, far, y):
    return jnp.where(y == 0, jnp.stack([x, far]), jnp.stack([far, x]))


def by_x(x, far, x_at):
    blocks = {0: x}
    for shift, block in zip(SHIFTS, far):
        blocks[-shift % 4] = block
    rows = []
    for k in range(4):
        off = (k - x_at) % 4
        rows.append(jnp.where(off < 2, jnp.where(off == 0, blocks[0], blocks[1]), jnp.where(off == 2, blocks[2], blocks[3])))
    return jnp.stack(rows)


def pix_gather(a, b):
    place = lax.axis_index("pix")
    y, x_at = place // 4, place % 4
    a_far = swap_pix(a)
    b_far = [turn_pix(b, shift) for shift in SHIFTS]
    a = by_y(a, a_far, y)
    b = by_x(b, b_far, x_at)
    b_far = swap_pix(b)
    a_far = [turn_pix(a, shift) for shift in SHIFTS]
    a = by_x(a, a_far, x_at).swapaxes(0, 1)
    b = by_y(b, b_far, y)
    return jnp.concatenate([a.reshape(-1, a.shape[-1]), b.reshape(-1, b.shape[-1])], axis=1)


def planes(matrix, slm):
    width = slm.shape[1] // 2
    pix, modes = matrix.shape[1:]
    times = mm(matrix.reshape(2 * pix, modes), slm, NN)
    return pair(times[:pix], times[pix:], width, 1.0)


def body(matrix, calibration_fields, patterns, targets, phases):
    pix_rows, mode_cols = matrix.shape[1:]
    pix_total = pix_rows * lax.axis_size("pix")
    mode_total = mode_cols * lax.axis_size("mode")
    width = targets.shape[1]
    floor_value = 0.5 * math.sqrt(pix_total / mode_total)

    fields = jnp.concatenate([calibration_fields[0].T, calibration_fields[1].T], axis=0)
    copies = jnp.broadcast_to(fields[None], (8,) + fields.shape)
    half = lax.all_to_all(copies, "mode", 0, 0, axis_index_groups=core_groups())
    core = lax.axis_index("mode") % 2
    rest = swap_cores(half)
    wave_high, wave_low, slm, panel_sum = wave(patterns, phases)

    row = (core * 8 + lax.axis_index("mode") // 2) * (pix_rows // 16)
    amplitude = lax.dynamic_slice_in_dim(targets, row, pix_rows // 16, 0).astype(jnp.float32) / 128.0

    seen = planes(matrix, slm)
    seen, high, low = first(1.0 / math.sqrt(mode_total), core.reshape(1), half, rest, panel_sum, seen)
    parts = None
    for part in range(UPDATES):
        parts = update(matrix, high, low, wave_high, wave_low, part, parts)
    updated, updated_turned = parts

    for repeat in range(ITERS + 1):
        if repeat > 0:
            seen = planes(updated, slm)
        seen = mode_scatter(seen)
        if repeat == ITERS:
            seen = mode_gather(seen)
            break
        seen = mode_gather(scaled(seen, amplitude * clamp_scale(seen, 0.5, width)))
        real, imag = seen[:, :width], seen[:, width:]
        both = jnp.concatenate([seen, jnp.concatenate([imag, -real], axis=1)], axis=0)
        real, imag = pix_scatter(mm(updated_turned, both, NN))
        factor = 1.0 / jnp.maximum(jnp.sqrt(real * real + imag * imag), floor_value)
        slm = pix_gather(real * factor, imag * factor)
    slm_field = jnp.stack([slm[:, :width], slm[:, width:]])
    camera_field = jnp.stack([seen[:, :width], seen[:, width:]])
    return (updated, slm_field, camera_field)


def solution(mesh):
    in_specs = (
        P(None, "pix", "mode"),
        P(None, "pix", "mode"),
        P("mode", None),
        P("pix", None),
        P("mode", None),
    )
    out_specs = (P(None, "pix", "mode"), P(None, "mode", None), P(None, "pix", None))
    return jax.shard_map(body, mesh=mesh, in_specs=in_specs, out_specs=out_specs, check_vma=False)
```
